32 devices in a mesh: rows: 32 (over z, y, x, core).
Axes of the slice: x: 2, y: 2, z: 4, core: 2. Of those that a mesh axis runs over, the one named last changes fastest.
Arguments:
- green_tile: float32 [32768, 2048], P('rows'), may hold values from -0.25 to 0.25
- charges: float32 [32768, 64], P('rows'), may hold values from -6 to 6
- background: float32 [32768, 64], P('rows'), may hold values from -6 to 6
- labels: int32 [32768], P('rows'), may hold values from 0 to 63
- slab_columns: int32 [2048], P('rows'), may hold values from 0 to 32767, as said below
Outputs:
- residual: float32 [32768, 64], P('rows')
- slab_gradient: float32 [2048, 64], P('rows')
The draws below stay inside these ranges and needn't reach their ends.
Inputs may be any that keep to these rules, and one draw needn't show every extreme that they name: `slab_columns`: slab column j is a panel among the rows of device j // 64; no panel appears twice; every device's 64 columns include its first and its last panel.
All inputs are finite; a program needn't handle non-finite values.
Results may differ from the reference program's by a relative error of at most 0.000065.
Values sent between devices are 32-bit elements; how exact they have to be, the bound alone decides.
No kernel may reach another device: no remote copies, remote signals or barrier semaphores. Data moves between devices by JAX's collectives and lax.ppermute only.
A program may use at most 64 MiB of HBM per device.

```python
import jax
import jax.numpy as jnp
from jax import lax

ROWS_DEV = 1024
SLAB = 2048
EXC = 64
PANELS = 32768
SLAB_DEV = 64
N_ROWS = 32


def draw_slab_columns(key, part):
    block_keys = jax.random.split(key, N_ROWS)

    def one_block(block_key, block):
        inner = jax.random.permutation(jax.random.fold_in(block_key, 1), ROWS_DEV - 2)[:SLAB_DEV - 2] + 1
        picked = jnp.concatenate([jnp.array([0, ROWS_DEV - 1], jnp.int32), inner.astype(jnp.int32)])
        order = jax.random.permutation(jax.random.fold_in(block_key, 2), SLAB_DEV)
        return picked[order] + block * ROWS_DEV
    blocks = jax.vmap(one_block)(block_keys, jnp.arange(N_ROWS, dtype=jnp.int32))
    return blocks.reshape(SLAB).astype(jnp.int32)


def touch_ends(values, own_key, smallest, high):
    shape = values.shape
    spot = [jax.random.randint(jax.random.fold_in(own_key, axis), (), 0, shape[axis]) for axis in range(len(shape))]
    values = values.at[tuple(spot)].set(smallest)
    longest = shape.index(max(shape))
    spot[longest] = (spot[longest] + 1) % shape[longest]
    return values.at[tuple(spot)].set(high)


def spiked(values, key, source, target, shards_of, factor):
    owner, partner = [(jnp.arange(values.shape[dim]) // (values.shape[dim] // shards_of)).reshape([-1 if axis == dim else 1 for axis in range(values.ndim)]) for dim in (source, target)]
    chosen = jax.random.permutation(key, shards_of)[partner]
    strong = (owner == chosen) | (owner == (partner + shards_of // 2) % shards_of)
    return jnp.where(strong, factor * values, values)


def level_of(key, extent, cuts, least, high):
    level = 1.0
    for position, blocks in cuts:
        steps = jax.random.uniform(jax.random.fold_in(jax.random.fold_in(key, 6), position), (blocks,), jnp.float32, least / len(cuts), high / len(cuts))
        level = level * jnp.repeat(jnp.exp(steps), extent[position] // blocks).reshape((-1,) + (1,) * (len(extent) - 1 - position))
    return level


def normal_values(own_key, extent, deviation, bound, cuts=(), kind=jnp.bfloat16):
    values = deviation * jax.random.normal(own_key, extent, jnp.float32)
    if cuts:
        values = values * level_of(own_key, extent, cuts, -0.22, 0.18)
    return jnp.clip(values, -bound, bound).astype(kind)


def heavy_noise(key, extent, width, bound, shards, heavy, held_as=jnp.bfloat16):
    values = width * jax.random.normal(key, extent, jnp.float32)
    if shards:
        values = values * level_of(key, extent, shards, -0.22, 0.18)
    return jnp.clip(spiked(values, jax.random.fold_in(key, 3), *heavy), -bound, bound).astype(held_as)


def setup_inputs(seed: int = 0) -> dict:
    streams_of = jax.random.split(jax.random.key(seed), 6)
    return {
        "green_tile": heavy_noise(streams_of[0], (PANELS, SLAB), SLAB ** -0.5, 0.25, ((0, 32),), (0, 1, 32, 2.75), jnp.float32),
        "charges": normal_values(streams_of[1], (PANELS, EXC), 1.0, 6.0, ((0, 32),), jnp.float32),
        "background": normal_values(streams_of[2], (PANELS, EXC), 1.0, 6.0, ((0, 32),), jnp.float32),
        "labels": touch_ends(jax.random.randint(streams_of[3], (PANELS,), 0, EXC), jax.random.fold_in(streams_of[3], 1), 0, EXC - 1).astype(jnp.int32),
        "slab_columns": draw_slab_columns(jax.random.fold_in(streams_of[5], 71), 0),
    }


def reference(green_tile, charges, background, labels, slab_columns):
    slab_charges = charges[slab_columns.astype(jnp.int32)]
    potential = jnp.dot(green_tile, slab_charges, preferred_element_type=jnp.float32, precision=lax.Precision.HIGHEST)
    target = (labels[:, None] == jnp.arange(EXC, dtype=jnp.int32)[None, :]).astype(jnp.float32)
    residual = background + potential - target
    slab_gradient = lax.dot_general(green_tile, residual, (((0,), (0,)), ((), ())), precision=lax.Precision.HIGHEST, preferred_element_type=jnp.float32)
    return residual, slab_gradient
```

```python
import jax
import jax.numpy as jnp
from jax import lax
from jax.experimental import pallas as pl
from jax.experimental.pallas import tpu as pltpu
from jax.sharding import PartitionSpec as P


LANES = 128
BLOCK = 256


def plain(green_tile, charges, background, labels, slab_columns):
    panel_count = green_tile.shape[0]
    owned_count = slab_columns.shape[0]
    first_panel = lax.axis_index("rows") * panel_count
    owned_charges = charges[slab_columns - first_panel]
    potential = jnp.dot(
        green_tile,
        lax.all_gather(owned_charges, "rows", axis=0, tiled=True),
        preferred_element_type=jnp.float32,
        precision=lax.Precision.HIGHEST,
    )
    target = (labels[:, None] == jnp.arange(charges.shape[1], dtype=jnp.int32)[None, :]).astype(
        jnp.float32
    )
    residual = background + potential - target
    partial_terms = lax.dot_general(
        green_tile,
        residual,
        (((0,), (0,)), ((), ())),
        precision=lax.Precision.HIGHEST,
        preferred_element_type=jnp.float32,
    )
    summed_terms = lax.psum(partial_terms, "rows")
    slab_gradient = lax.dynamic_slice_in_dim(
        summed_terms, lax.axis_index("rows") * owned_count, owned_count, 0
    )
    return (residual, slab_gradient)


def two_halves(values):
    high = values.astype(jnp.bfloat16)
    low = (values - high.astype(jnp.float32)).astype(jnp.bfloat16)
    return high, low


def gather_kernel(charges_ref, columns_ref, out_ref):
    exc, panels = charges_ref.shape
    half = exc // 2
    columns = columns_ref[...] - lax.axis_index("rows") * panels
    columns = jnp.concatenate([columns, columns], axis=1)
    picked = (
        lax.broadcasted_iota(jnp.int32, (panels, LANES), 0) == columns
    ).astype(jnp.float32).astype(jnp.bfloat16)
    values = charges_ref[...]
    high = values.astype(jnp.bfloat16)
    rest = values - high.astype(jnp.float32)
    middle, low = two_halves(rest)
    pieces = jnp.dot(
        jnp.concatenate([high, middle, low], axis=0),
        picked,
        preferred_element_type=jnp.float32,
    )
    taken = pieces[:exc] + pieces[exc : 2 * exc] + pieces[2 * exc :]
    lane = lax.broadcasted_iota(jnp.int32, (half, LANES), 1)
    out_ref[...] = jnp.where(lane < LANES // 2, taken[:half], taken[half:])


def products_kernel(
    green_ref, own_ref, other_ref, background_ref, labels_ref,
    residual_ref, send_ref, keep_ref, stack, high_ref, low_ref,
):
    panels, slab = green_ref.shape
    exc = background_ref.shape[0]
    half = exc // 2
    chips = own_ref.shape[0]
    me = lax.axis_index("rows")
    core = lax.rem(me, 2)
    chip = lax.div(me, 2)
    first = core == 0
    lane = lax.broadcasted_iota(jnp.int32, (half, LANES), 1) < LANES // 2
    for r in range(chips):
        own, other = own_ref[r], other_ref[r]
        even = jnp.where(first, own, other)
        odd = jnp.where(first, other, own)
        lower = jnp.where(lane, even, pltpu.roll(odd, LANES // 2, 1))
        upper = jnp.where(lane, pltpu.roll(even, LANES // 2, 1), odd)
        high, low = two_halves(jnp.concatenate([lower, upper], axis=0))
        place = pl.ds(pl.multiple_of(jnp.bitwise_xor(chip, r) * LANES, LANES), LANES)
        stack[:exc, place] = high
        stack[exc:, place] = low
    numbers = lax.broadcasted_iota(jnp.int32, (exc, BLOCK), 0)
    total = None
    for b in range(panels // BLOCK):
        rows = slice(b * BLOCK, (b + 1) * BLOCK)
        high, low = two_halves(green_ref[rows, :])
        contract = (((1,), (1,)), ((), ()))
        pot = lax.dot_general(
            stack[...], high, contract, preferred_element_type=jnp.float32
        ) + lax.dot_general(stack[...], low, contract, preferred_element_type=jnp.float32)
        pot = pot[:exc] + pot[exc:]
        target = (labels_ref[:, rows] == numbers).astype(jnp.float32)
        residual = background_ref[:, rows] + pot - target
        residual_ref[:, rows] = residual
        res = jnp.concatenate(two_halves(residual), axis=0)
        terms = jnp.dot(res, high, preferred_element_type=jnp.float32) + jnp.dot(
            res, low, preferred_element_type=jnp.float32
        )
        terms = terms[:exc] + terms[exc:]
        total = terms if total is None else total + terms
    for d in range(chips):
        r = jnp.bitwise_xor(chip, d)
        rz, rq = lax.div(r, 4), lax.rem(r, 4)
        lower = total[:half, d * LANES : (d + 1) * LANES]
        upper = total[half:, d * LANES : (d + 1) * LANES]
        keep_ref[rq, rz] = jnp.where(first, lower, upper)
        send_ref[rq, rz] = jnp.where(first, upper, lower)


def finish_kernel(mine_ref, other_ref, out_ref, turned):
    core = lax.rem(lax.axis_index("rows"), 2)
    first = core == 0
    owned = out_ref.shape[0]
    mine, other = mine_ref[...], other_ref[...]
    lower = jnp.where(first, mine, other)
    upper = jnp.where(first, other, mine)
    turned[...] = jnp.concatenate([lower, upper], axis=0).T
    out_ref[...] = turned[pl.ds(pl.multiple_of(core * owned, owned), owned), :]


def local(green_tile, charges, background, labels, slab_columns):
    panels, slab = green_tile.shape
    exc = charges.shape[1]
    half = exc // 2
    owned = slab_columns.shape[0]
    n = slab // owned
    chips = n // 2

    def swap(value, mask):
        return lax.ppermute(value, "rows", [(i, i ^ mask) for i in range(n)])

    vmem = pl.BlockSpec(memory_space=pltpu.VMEM)
    f32 = jnp.float32
    chunk = pl.pallas_call(
        gather_kernel,
        out_shape=jax.ShapeDtypeStruct((half, LANES), f32),
        in_specs=[vmem, vmem],
        out_specs=vmem,
        name="gather",
    )(charges.T, slab_columns.reshape(1, owned))
    along_z = jnp.stack([chunk] + [swap(chunk, k * 8) for k in range(1, 4)])
    quads = jnp.stack([along_z] + [swap(along_z, k * 2) for k in range(1, 4)], axis=1)
    own = quads.reshape(chips, half, LANES)
    other = swap(own, 1)
    part = jax.ShapeDtypeStruct((4, 4, half, LANES), f32)
    residual, send, keep = pl.pallas_call(
        products_kernel,
        out_shape=(jax.ShapeDtypeStruct((exc, panels), f32), part, part),
        in_specs=[vmem] * 5,
        out_specs=(vmem,) * 3,
        scratch_shapes=[
            pltpu.VMEM((2 * exc, slab), jnp.bfloat16),
            pltpu.VMEM((8, LANES), jnp.bfloat16),
            pltpu.VMEM((8, LANES), jnp.bfloat16),
        ],
        compiler_params=pltpu.CompilerParams(vmem_limit_bytes=40 << 20),
        name="products",
    )(green_tile, own, other, background.T, labels.reshape(1, panels))
    halves = keep + swap(send, 1)
    quarter = halves[0]
    for k in range(1, 4):
        quarter = quarter + swap(halves[k], k * 2)
    mine = quarter[0]
    for k in range(1, 4):
        mine = mine + swap(quarter[k], k * 8)
    slab_gradient = pl.pallas_call(
        finish_kernel,
        out_shape=jax.ShapeDtypeStruct((owned, exc), f32),
        in_specs=[vmem, vmem],
        out_specs=vmem,
        scratch_shapes=[pltpu.VMEM((LANES, exc), f32)],
        name="finish",
    )(mine, swap(mine, 1))
    return residual.T, slab_gradient


def solution(mesh):
    placed = (P("rows", None), P("rows", None), P("rows", None), P("rows"), P("rows"))

    def program(green_tile, charges, background, labels, slab_columns):
        fits = mesh.shape["rows"] == 32 and slab_columns.shape[0] == 32 * 64
        return jax.shard_map(
            local if fits else plain,
            mesh=mesh,
            in_specs=placed,
            out_specs=(P("rows", None), P("rows", None)),
            check_vma=False,
        )(green_tile, charges, background, labels, slab_columns)

    return program
```

```python
import jax
import jax.numpy as jnp
from jax import lax
from jax.experimental import pallas as pl
from jax.experimental.pallas import tpu as pltpu
from jax.sharding import PartitionSpec as P


LANES = 128
BLOCK = 128


def plain(green_tile, charges, background, labels, slab_columns):
    panel_count = green_tile.shape[0]
    owned_count = slab_columns.shape[0]
    first_panel = lax.axis_index("rows") * panel_count
    owned_charges = charges[slab_columns - first_panel]
    potential = jnp.dot(
        green_tile,
        lax.all_gather(owned_charges, "rows", axis=0, tiled=True),
        preferred_element_type=jnp.float32,
        precision=lax.Precision.HIGHEST,
    )
    target = (labels[:, None] == jnp.arange(charges.shape[1], dtype=jnp.int32)[None, :]).astype(
        jnp.float32
    )
    residual = background + potential - target
    partial_terms = lax.dot_general(
        green_tile,
        residual,
        (((0,), (0,)), ((), ())),
        precision=lax.Precision.HIGHEST,
        preferred_element_type=jnp.float32,
    )
    summed_terms = lax.psum(partial_terms, "rows")
    slab_gradient = lax.dynamic_slice_in_dim(
        summed_terms, lax.axis_index("rows") * owned_count, owned_count, 0
    )
    return (residual, slab_gradient)


def two_halves(values):
    high = values.astype(jnp.bfloat16)
    low = (values - high.astype(jnp.float32)).astype(jnp.bfloat16)
    return high, low


def matmul(left, right, axis):
    contract = (((1,), (axis,)), ((), ()))
    return lax.dot_general(left, right, contract, preferred_element_type=jnp.float32)


def gather_kernel(charges_hbm, columns_hbm, out_ref, charges_ref, columns_ref, arrived):
    fetch_columns = pltpu.make_async_copy(columns_hbm, columns_ref, arrived.at[0])
    fetch_charges = pltpu.make_async_copy(charges_hbm, charges_ref, arrived.at[1])
    fetch_columns.start()
    fetch_charges.start()
    exc, panels = charges_ref.shape
    fetch_columns.wait()
    half = exc // 2
    columns = columns_ref[...] - lax.axis_index("rows") * panels
    columns = jnp.concatenate([columns, columns], axis=1)
    picked = (
        lax.broadcasted_iota(jnp.int32, (panels, LANES), 0) == columns
    ).astype(jnp.float32).astype(jnp.bfloat16)
    fetch_charges.wait()
    values = charges_ref[...]
    high = values.astype(jnp.bfloat16)
    rest = values - high.astype(jnp.float32)
    middle, low = two_halves(rest)
    pieces = jnp.dot(
        jnp.concatenate([high, middle, low], axis=0),
        picked,
        preferred_element_type=jnp.float32,
    )
    taken = pieces[:exc] + pieces[exc : 2 * exc] + pieces[2 * exc :]
    lane = lax.broadcasted_iota(jnp.int32, (half, LANES), 1)
    chunk = jnp.where(lane < LANES // 2, taken[:half], taken[half:])
    for chip in range(out_ref.shape[0]):
        out_ref[chip] = chunk


def products_kernel(
    green_hbm, own_ref, other_ref, background_hbm, labels_hbm,
    residual_ref, send_ref, keep_ref,
    stack, green_ref, background_ref, labels_ref, green_in, small_in,
):
    panels, slab = green_ref.shape
    blocks = [slice(b * BLOCK, (b + 1) * BLOCK) for b in range(panels // BLOCK)]
    fetch_green = [
        pltpu.make_async_copy(green_hbm.at[rows], green_ref.at[rows], green_in.at[b])
        for b, rows in enumerate(blocks)
    ]
    fetch_small = [
        pltpu.make_async_copy(background_hbm, background_ref, small_in.at[0]),
        pltpu.make_async_copy(labels_hbm, labels_ref, small_in.at[1]),
    ]
    exc = background_ref.shape[0]
    half = exc // 2
    chips = own_ref.shape[0]
    fetch_green[0].start()
    for copy in fetch_small:
        copy.start()
    fetch_green[1].start()
    first = lax.rem(lax.axis_index("rows"), 2) == 0
    lane = lax.broadcasted_iota(jnp.int32, (half, LANES), 1) < LANES // 2
    for d in range(chips):
        own, other = own_ref[d], other_ref[d]
        even = jnp.where(first, own, other)
        odd = jnp.where(first, other, own)
        lower = jnp.where(lane, even, pltpu.roll(odd, LANES // 2, 1))
        upper = jnp.where(lane, pltpu.roll(even, LANES // 2, 1), odd)
        high, low = two_halves(jnp.concatenate([lower, upper], axis=0))
        place = slice(d * LANES, (d + 1) * LANES)
        stack[:exc, place] = high
        stack[exc:, place] = low
    numbers = lax.broadcasted_iota(jnp.int32, (exc, BLOCK), 0)
    total = None

    def transposed(total, high, low, res_high, res_low):
        terms = matmul(jnp.concatenate([res_high, res_low], axis=0), high, 0)
        terms = terms[:exc] + terms[exc:] + matmul(res_high, low, 0)
        return terms if total is None else total + terms

    held = None
    for b, rows in enumerate(blocks):
        fetch_green[b].wait()
        if b + 2 < len(blocks):
            fetch_green[b + 2].start()
        if b == 0:
            for copy in fetch_small:
                copy.wait()
        high, low = two_halves(green_ref[rows, :])
        pot = matmul(stack[...], high, 1)
        pot = pot[:exc] + pot[exc:] + matmul(stack[:exc, :], low, 1)
        if held is not None:
            total = transposed(total, *held)
        target = (labels_ref[:, rows] == numbers).astype(jnp.float32)
        residual = background_ref[:, rows] + pot - target
        residual_ref[:, rows] = residual
        held = (high, low) + two_halves(residual)
    total = transposed(total, *held)
    for d in range(chips):
        lower = total[:half, d * LANES : (d + 1) * LANES]
        upper = total[half:, d * LANES : (d + 1) * LANES]
        even = jnp.where(lane, lower, pltpu.roll(upper, LANES // 2, 1))
        odd = jnp.where(lane, pltpu.roll(lower, LANES // 2, 1), upper)
        keep_ref[d] = jnp.where(first, even, odd)
        send_ref[d] = jnp.where(first, odd, even)


def finish_kernel(terms_ref, out_ref):
    owned = out_ref.shape[0]
    summed = terms_ref[0]
    for d in range(1, terms_ref.shape[0]):
        summed = summed + terms_ref[d]
    out_ref[...] = jnp.concatenate([summed[:, :owned], summed[:, owned:]], axis=0).T


def local(green_tile, charges, background, labels, slab_columns):
    panels, slab = green_tile.shape
    exc = charges.shape[1]
    half = exc // 2
    owned = slab_columns.shape[0]
    n = slab // owned
    chips = n // 2
    cores = [list(range(core, n, 2)) for core in range(2)]
    partners = [(i, i ^ 1) for i in range(n)]

    def in_hbm(value):
        return pltpu.with_memory_space_constraint(value, pltpu.HBM)

    def across(value):
        return lax.all_to_all(value, "rows", 0, 0, axis_index_groups=cores, tiled=True)

    vmem = pl.BlockSpec(memory_space=pltpu.VMEM)
    hbm = pl.BlockSpec(memory_space=pltpu.HBM)
    f32 = jnp.float32
    chunks = jax.ShapeDtypeStruct((chips, half, LANES), f32)
    small = pltpu.CompilerParams(vmem_limit_bytes=8 << 20)
    copies = pl.pallas_call(
        gather_kernel,
        out_shape=chunks,
        in_specs=[hbm, hbm],
        out_specs=vmem,
        scratch_shapes=[
            pltpu.VMEM((exc, panels), f32),
            pltpu.VMEM((1, owned), jnp.int32),
            pltpu.SemaphoreType.DMA((2,)),
        ],
        compiler_params=small,
        name="gather",
    )(in_hbm(charges.T), in_hbm(slab_columns.reshape(1, owned)))
    own = across(copies)
    other = lax.ppermute(own, "rows", partners)
    residual, send, keep = pl.pallas_call(
        products_kernel,
        out_shape=(jax.ShapeDtypeStruct((exc, panels), f32), chunks, chunks),
        in_specs=[hbm, vmem, vmem, hbm, hbm],
        out_specs=(vmem,) * 3,
        scratch_shapes=[
            pltpu.VMEM((2 * exc, slab), jnp.bfloat16),
            pltpu.VMEM((panels, slab), f32),
            pltpu.VMEM((exc, panels), f32),
            pltpu.VMEM((1, panels), jnp.int32),
            pltpu.SemaphoreType.DMA((panels // BLOCK,)),
            pltpu.SemaphoreType.DMA((2,)),
        ],
        compiler_params=pltpu.CompilerParams(vmem_limit_bytes=40 << 20),
        name="products",
    )(in_hbm(green_tile), own, other, in_hbm(background.T), in_hbm(labels.reshape(1, panels)))
    slab_gradient = pl.pallas_call(
        finish_kernel,
        out_shape=jax.ShapeDtypeStruct((owned, exc), f32),
        in_specs=[vmem],
        out_specs=vmem,
        compiler_params=small,
        name="finish",
    )(across(keep + lax.ppermute(send, "rows", partners)))
    return residual.T, slab_gradient


def solution(mesh):
    placed = (P("rows", None), P("rows", None), P("rows", None), P("rows"), P("rows"))

    def program(green_tile, charges, background, labels, slab_columns):
        fits = mesh.shape["rows"] == 32 and slab_columns.shape[0] == 32 * 64
        return jax.shard_map(
            local if fits else plain,
            mesh=mesh,
            in_specs=placed,
            out_specs=(P("rows", None), P("rows", None)),
            check_vma=False,
        )(green_tile, charges, background, labels, slab_columns)

    return program
```
